128 devices in a mesh: row: 8 (over x_lo, z), col: 16 (over y, x_hi, core).
Axes of the slice: x: 4 (x_hi: 2, x_lo: 2; x = x_hi * 2 + x_lo), y: 4, z: 4, core: 2. Of those that a mesh axis runs over, the one named last changes fastest.
Arguments:
- tokens: bfloat16 [1024, 12288], P('col', 'row'), may hold values from -6 to 6
- up_weight: bfloat16 [12288, 24576], P('row', 'col'), may hold values from -0.109375 to 0.109375
- up_mask: int32 [192, 384], P('row', 'col'), may hold values 0 or 1
- down_weight: bfloat16 [24576, 12288], P('col', 'row'), may hold values from -0.078125 to 0.078125
- down_mask: int32 [384, 192], P('col', 'row'), may hold values 0 or 1
- grad_out: bfloat16 [1024, 12288], P('col', 'row'), may hold values from -6 to 6
Outputs:
- out_heads: bfloat16 [96, 1024, 128], P('row', 'col')
- grad_tokens: bfloat16 [1024, 12288], P('col', 'row')
- grad_up: bfloat16 [12288, 24576], P('row', 'col')
- grad_down: bfloat16 [24576, 12288], P('col', 'row')
The draws below stay inside these ranges and needn't reach their ends.
All inputs are finite; a program needn't handle non-finite values. No bound on the sum of `up_mask` or of `down_mask` on one device may be relied on, other than what follows from the above.
Results may differ from the reference program's by a relative error of at most 0.022.
Values may be sent and summed in bfloat16 or wider, within the bound.
A program may use at most 192 MiB of HBM per device.

```python
import math
import jax
import jax.numpy as jnp
from jax import lax

D = 12288
FF = 24576
BLOCK = 64
HEAD_DIM = 128
HEADS = 96
TOKENS = 1024
N_ROW = 8
N_COL = 16


def with_ends(entries, stream_key, least, largest):
    place = [jax.random.randint(jax.random.fold_in(stream_key, axis), (), 0, length) for axis, length in enumerate(entries.shape)]
    widest = entries.shape.index(max(entries.shape))
    neighbour = place[:widest] + [(place[widest] + 1) % entries.shape[widest]] + place[widest + 1:]
    return entries.at[tuple(place)].set(least).at[tuple(neighbour)].set(largest)


def levels(own_key, extent, pieces, low, top_value):
    loudness = 1.0
    for axis_at, blocks in pieces:
        steps = jax.random.uniform(jax.random.fold_in(jax.random.fold_in(own_key, 6), axis_at), (blocks,), jnp.float32, low / len(pieces), top_value / len(pieces))
        loudness = loudness * jnp.repeat(jnp.exp(steps), extent[axis_at] // blocks).reshape((-1,) + (1,) * (len(extent) - 1 - axis_at))
    return loudness


def centred(rng, dims, spread, reach, pieces=(), kind=jnp.bfloat16):
    loudness = levels(rng, dims, pieces, -0.22, 0.18) if pieces else 1.0
    array = jax.random.normal(rng, dims, jnp.float32) * spread * loudness
    return jnp.minimum(jnp.maximum(array, -reach), reach).astype(kind)


def setup_inputs(seed: int = 0) -> dict:
    splits = jax.random.split(jax.random.key(seed), 7)
    return {
        "tokens": centred(splits[0], (TOKENS, D), 1.0, 6.0, ((0, 16), (1, 8))),
        "up_weight": centred(splits[1], (D, FF), (D // 4) ** -0.5, 0.109375, ((0, 8), (1, 16))),
        "up_mask": with_ends((jax.random.randint(splits[2], (D // BLOCK, FF // BLOCK), 0, 4) < 1).astype(jnp.int32), jax.random.fold_in(splits[2], 1), 0, 1),
        "down_weight": centred(splits[3], (FF, D), (FF // 4) ** -0.5, 0.078125, ((0, 16), (1, 8))),
        "down_mask": with_ends((jax.random.randint(splits[4], (FF // BLOCK, D // BLOCK), 0, 4) < 1).astype(jnp.int32), jax.random.fold_in(splits[4], 1), 0, 1),
        "grad_out": centred(splits[5], (TOKENS, D), 1.0, 6.0, ((0, 16), (1, 8))),
    }


def expand(weight, mask):
    rows_in, cols_in = weight.shape
    tiles = weight.reshape(rows_in // BLOCK, BLOCK, cols_in // BLOCK, BLOCK)
    tiles = tiles * mask.astype(weight.dtype)[:, None, :, None]
    return tiles.reshape(rows_in, cols_in)

def activate(value):
    return jax.nn.gelu(value, approximate=True)

def block_sum(left, right, groups, right_t):
    width = left.shape[1] // groups
    acc = None
    for group in range(groups):
        piece = left[:, group * width:(group + 1) * width]
        if right_t:
            other = right[:, group * width:(group + 1) * width]
            term = lax.dot_general(piece, other, (((1,), (1,)), ((), ())), preferred_element_type=jnp.float32)
        else:
            other = right[group * width:(group + 1) * width, :]
            term = jnp.dot(piece, other, preferred_element_type=jnp.float32)
        term = term.astype(jnp.bfloat16).astype(jnp.float32)
        acc = term if acc is None else acc + term
    return acc

def reference(tokens, up_weight, up_mask, down_weight, down_mask, grad_out):
    w_up = expand(up_weight, up_mask)
    w_down = expand(down_weight, down_mask)
    pre_act = block_sum(tokens, w_up, N_ROW, False)
    hidden = activate(pre_act).astype(jnp.bfloat16)
    output = block_sum(hidden, w_down, N_COL, False).astype(jnp.bfloat16)
    out_heads = output.reshape(TOKENS, HEADS, HEAD_DIM).transpose(1, 0, 2)
    grad_hidden = block_sum(grad_out, w_down, N_ROW, True)
    unused, pull = jax.vjp(activate, pre_act)
    grad_pre = pull(grad_hidden)[0].astype(jnp.bfloat16)
    grad_scale = 1.0 / math.sqrt(TOKENS)
    grad_up = lax.dot_general(tokens, grad_pre, (((0,), (0,)), ((), ())), preferred_element_type=jnp.float32)
    grad_up = expand(grad_up * grad_scale, up_mask).astype(jnp.bfloat16)
    grad_down = lax.dot_general(hidden, grad_out, (((0,), (0,)), ((), ())), preferred_element_type=jnp.float32)
    grad_down = expand(grad_down * grad_scale, down_mask).astype(jnp.bfloat16)
    grad_tokens = block_sum(grad_pre, w_up, N_COL, True).astype(jnp.bfloat16)
    return (out_heads, grad_tokens, grad_up, grad_down)
```

```python
import functools
import math

import jax
import jax.numpy as jnp
from jax import lax
from jax.experimental import pallas as pl
from jax.experimental.pallas import tpu as pltpu
from jax.sharding import PartitionSpec as P

BLOCK = 64
HEAD_DIM = 128
CHUNKS = 4
TILE = 256
MESH = pl.DeviceIdType.MESH
F32 = jnp.float32
BF16 = jnp.bfloat16

AG_XH, AG_Y, AG_CORE = 0, 1, 4
A_X, A_Z, B_Z, B_X = 5, 6, 9, 12
C_X, C_Z, D_Z, D_X = 13, 14, 17, 20
R_CORE, R_Y, R_XH = 21, 22, 25
MESSAGES = 26


def dot_nn(left, right):
    return jnp.dot(left, right, preferred_element_type=F32)


def dot_nt(left, right):
    return lax.dot_general(left, right, (((1,), (1,)), ((), ())), preferred_element_type=F32)


def dot_tn(left, right):
    return lax.dot_general(left, right, (((0,), (0,)), ((), ())), preferred_element_type=F32)


def tile_at(index):
    return pl.ds(pl.multiple_of(index * TILE, TILE), TILE)


def kernel(
    tok, wup, mup, wdn, mdn, cot,
    oh, gt, gu, gd,
    tc, wu, wd, m2u, m2d, pa, pb, ra, rb, sb, sbo, r3a, r3b, hid, gra, out, r7a, r7b, s8, r7c,
    ss, rs, ls,
):
    width = tok.shape[1]
    tokens = tc.shape[0]
    chunk = tokens // CHUNKS
    piece = tok.shape[0] // CHUNKS
    tiles = width // TILE
    grad_scale = 1.0 / math.sqrt(tokens)

    row, col = lax.axis_index("row"), lax.axis_index("col")
    xl, z = row // 4, row % 4
    y, xh, k = col // 4, (col // 2) % 2, col % 2

    def device(xl=xl, z=z, y=y, xh=xh, k=k):
        return (xl * 4 + z, y * 4 + xh * 2 + k)

    z_to = [(z + d) % 4 for d in (1, 2, 3)]
    z_from = [(z + 4 - d) % 4 for d in (1, 2, 3)]
    y_to = [(y + d) % 4 for d in (1, 2, 3)]
    y_from = [(y + 4 - d) % 4 for d in (1, 2, 3)]
    x_dev, xh_dev, core_dev = device(xl=1 - xl), device(xh=1 - xh), device(k=1 - k)
    z_dev = [device(z=v) for v in z_to]
    y_dev = [device(y=v) for v in y_to]

    def rows_of(j, k_, y_, xh_, pieces):
        at = j * chunk + k_ * (chunk // 2) + y_ * (2 * piece) + xh_ * piece
        return pl.ds(pl.multiple_of(at, piece), pieces * piece)

    pending = []

    def send(j, i, src, dst, dev):
        copy = pltpu.make_async_remote_copy(
            src_ref=src, dst_ref=dst, send_sem=ss.at[j, i], recv_sem=rs.at[j, i],
            device_id=dev, device_id_type=MESH,
        )
        copy.start()
        pending.append(copy)

    def arrived(j, i, here, dev):
        pltpu.make_async_remote_copy(
            src_ref=here, dst_ref=here, send_sem=ss.at[j, i], recv_sem=rs.at[j, i],
            device_id=dev, device_id_type=MESH,
        ).wait_recv()

    own = []
    for j in range(CHUNKS):
        there = rows_of(j, k, y, xh, 1)
        here = pl.ds(j * piece, piece)
        pair = (
            pltpu.make_async_copy(tok.at[here], tc.at[there, pl.ds(0, width)], ls.at[2 * j]),
            pltpu.make_async_copy(cot.at[here], tc.at[there, pl.ds(width, width)], ls.at[2 * j + 1]),
        )
        for copy in pair:
            copy.start()
        own.append(pair)
    load_up = pltpu.make_async_copy(wup, wu, ls.at[2 * CHUNKS])
    load_dn = pltpu.make_async_copy(wdn, wd, ls.at[2 * CHUNKS + 1])
    load_up.start()
    load_dn.start()

    barrier = pltpu.get_barrier_semaphore()
    for dev in [x_dev, xh_dev, core_dev] + z_dev + y_dev:
        pl.semaphore_signal(barrier, inc=1, device_id=dev, device_id_type=MESH)
    pl.semaphore_wait(barrier, 9)

    def ag_x(j):
        for copy in own[j]:
            copy.wait()
        at = tc.at[rows_of(j, k, y, xh, 1)]
        send(j, AG_XH, at, at, xh_dev)

    def ag_y(j):
        arrived(j, AG_XH, tc.at[rows_of(j, k, y, 1 - xh, 1)], xh_dev)
        at = tc.at[rows_of(j, k, y, 0, 2)]
        for d in range(3):
            send(j, AG_Y + d, at, at, y_dev[d])

    def ag_core(j):
        for d in range(3):
            arrived(j, AG_Y + d, tc.at[rows_of(j, k, y_from[d], 0, 2)], y_dev[d])
        at = tc.at[rows_of(j, k, 0, 0, 8)]
        send(j, AG_CORE, at, at, core_dev)

    def up(j):
        arrived(j, AG_CORE, tc.at[rows_of(j, 1 - k, 0, 0, 8)], core_dev)
        rows = pl.ds(j * chunk, chunk)

        @pl.loop(0, tiles)
        def _(n):
            value = dot_nn(tc[rows, pl.ds(0, width)], wu[:, tile_at(n)]).astype(BF16)
            pa[j, :, :, :, tile_at(n)] = value.reshape(2, 4, chunk // 8, TILE)

        send(j, A_X, pa.at[j, 1 - xl], ra.at[j], x_dev)

        @pl.loop(0, tiles)
        def _(n):
            value = dot_nt(tc[rows, pl.ds(width, width)], wd[tile_at(n), :]).astype(BF16)
            pb[j, :, :, :, tile_at(n)] = value.reshape(2, 4, chunk // 8, TILE)

        for d in range(3):
            send(j, A_Z + d, pb.at[j, :, z_to[d]], rb.at[j, d], z_dev[d])

    def sum_a(j):
        arrived(j, A_X, ra.at[j], x_dev)

        @pl.loop(0, 4)
        def _(v):
            pa[j, xl, v] = (pa[j, xl, v].astype(F32) + ra[j, v].astype(F32)).astype(BF16)

        for d in range(3):
            send(j, B_Z + d, pa.at[j, xl, z_to[d]], r3a.at[j, d], z_dev[d])
        for d in range(3):
            arrived(j, A_Z + d, rb.at[j, d], z_dev[d])

        def total(v):
            value = pb[j, v, z].astype(F32)
            for d in range(3):
                value = value + rb[j, d, v].astype(F32)
            return value

        sb[j] = total(1 - xl).astype(BF16)
        send(j, B_X, sb.at[j], r3b.at[j], x_dev)
        sbo[j] = total(xl)

    def sum_b(j):
        for d in range(3):
            arrived(j, B_Z + d, r3a.at[j, d], z_dev[d])
        arrived(j, B_X, r3b.at[j], x_dev)
        pre = pa[j, xl, z].astype(F32)
        for d in range(3):
            pre = pre + r3a[j, d].astype(F32)
        back = sbo[j] + r3b[j].astype(F32)
        root = 0.7978845608028654
        square = pre * pre
        bend = jnp.tanh(root * (pre + 0.044715 * (square * pre)))
        half = 0.5 * (1.0 + bend)
        slope = half + 0.5 * pre * (1.0 - bend * bend) * (root * (1.0 + 3 * 0.044715 * square))
        hid[j, xl, z] = (pre * half).astype(BF16)
        gra[j, xl, z] = (back * slope).astype(BF16)
        for d in range(3):
            send(j, C_Z + d, gra.at[j, xl, z], gra.at[j, xl, z], z_dev[d])
        send(j, C_X, hid.at[j, xl, z], hid.at[j, xl, z], x_dev)

    def spread(j):
        arrived(j, C_X, hid.at[j, 1 - xl, z], x_dev)
        for d in range(3):
            send(j, D_Z + d, hid.at[j, :, z], hid.at[j, :, z], z_dev[d])
        for d in range(3):
            arrived(j, C_Z + d, gra.at[j, xl, z_from[d]], z_dev[d])
        send(j, D_X, gra.at[j, xl], gra.at[j, xl], x_dev)

    def down(j):
        for d in range(3):
            arrived(j, D_Z + d, hid.at[j, :, z_from[d]], z_dev[d])

        @pl.loop(0, tiles)
        def _(n):
            value = dot_nn(hid[j].reshape(chunk, width), wd[:, tile_at(n)]).astype(BF16)
            out[j, :, :, :, tile_at(n)] = value.reshape(2, 4, 2 * piece, TILE)

        arrived(j, D_X, gra.at[j, 1 - xl], x_dev)

        @pl.loop(0, tiles)
        def _(n):
            value = dot_nt(gra[j].reshape(chunk, width), wu[tile_at(n), :]).astype(BF16)
            out[j, :, :, :, tile_at(n + tiles)] = value.reshape(2, 4, 2 * piece, TILE)

        send(j, R_CORE, out.at[j, 1 - k], r7a.at[j], core_dev)

    def rs_core(j):
        arrived(j, R_CORE, r7a.at[j], core_dev)

        @pl.loop(0, 4)
        def _(v):
            out[j, k, v] = (out[j, k, v].astype(F32) + r7a[j, v].astype(F32)).astype(BF16)

        for d in range(3):
            send(j, R_Y + d, out.at[j, k, y_to[d]], r7b.at[j, d], y_dev[d])

    def rs_y(j):
        for d in range(3):
            arrived(j, R_Y + d, r7b.at[j, d], y_dev[d])
        value = out[j, k, y].astype(F32)
        for d in range(3):
            value = value + r7b[j, d].astype(F32)
        s8[j] = value.astype(BF16).reshape(2, piece, 2 * width)
        send(j, R_XH, s8.at[j, 1 - xh], r7c.at[j], xh_dev)

    def rs_x(j):
        arrived(j, R_XH, r7c.at[j], xh_dev)
        value = (s8[j, xh].astype(F32) + r7c[j].astype(F32)).astype(BF16)
        here = pl.ds(j * piece, piece)
        for head in range(width // HEAD_DIM):
            oh[head, here, :] = value[:, head * HEAD_DIM:(head + 1) * HEAD_DIM]
        gt[here, :] = value[:, width:]

    def weight_grad(left, right, mask, place, result, sem):
        @pl.loop(0, tiles)
        def _(m):
            @pl.loop(0, tiles)
            def _(n):
                value = dot_tn(left(tile_at(m)), right(tile_at(n))) * grad_scale
                for b in range(TILE // BLOCK):
                    keep = mask[pl.ds(m * (TILE // BLOCK) + b, 1), tile_at(n)]
                    part = value[b * BLOCK:(b + 1) * BLOCK] * keep
                    at = pl.ds(pl.multiple_of(m * TILE + b * BLOCK, BLOCK), BLOCK)
                    place[at, tile_at(n)] = part.astype(BF16)

        copy = pltpu.make_async_copy(place, result, sem)
        copy.start()
        return copy

    def grad_up():
        return weight_grad(
            lambda t: tc[:, t],
            lambda t: gra[:, :, :, :, t].reshape(tokens, TILE),
            m2u, wu, gu, ls.at[2 * CHUNKS + 2],
        )

    def grad_down():
        return weight_grad(
            lambda t: hid[:, :, :, :, t].reshape(tokens, TILE),
            lambda t: tc[:, pl.ds(pl.multiple_of(t.start + width, TILE), TILE)],
            m2d, wd, gd, ls.at[2 * CHUNKS + 3],
        )

    for j in range(CHUNKS):
        ag_x(j)
    for j in range(CHUNKS):
        ag_y(j)

    blocks = width // BLOCK
    at = lax.broadcasted_iota(jnp.int32, (blocks, width), 1)
    first = lax.broadcasted_iota(jnp.int32, (blocks, width), 0) * BLOCK
    repeat = jnp.where((at >= first) & (at < first + BLOCK), 1.0, 0.0).astype(F32)
    for mask, wide, weight, load in ((mup, m2u, wu, load_up), (mdn, m2d, wd, load_dn)):
        wide[...] = dot_nn(mask[...].astype(F32), repeat)
        load.wait()

        @pl.loop(0, blocks)
        def _(b):
            rows = pl.ds(pl.multiple_of(b * BLOCK, BLOCK), BLOCK)
            weight[rows, :] = (weight[rows, :].astype(F32) * wide[pl.ds(b, 1), :]).astype(BF16)

    for j in (0, 1):
        ag_core(j)
        up(j)
    for step in (sum_a, sum_b):
        for j in (0, 1):
            step(j)
    for j in (2, 3):
        ag_core(j)
    for j in (0, 1):
        spread(j)
    for j in (2, 3):
        up(j)
    for j in (0, 1):
        down(j)
    for j in (2, 3):
        sum_a(j)
    for j in (0, 1):
        rs_core(j)
    for j in (2, 3):
        sum_b(j)
    for j in (0, 1):
        rs_y(j)
    for j in (2, 3):
        spread(j)
    for j in (0, 1):
        rs_x(j)
    down(2)
    rs_core(2)
    down(3)
    stores = [grad_up()]
    rs_core(3)
    rs_y(2)
    stores.append(grad_down())
    rs_y(3)
    rs_x(2)
    rs_x(3)
    for copy in pending:
        copy.wait_send()
    for copy in stores:
        copy.wait()


def body(tokens, up_weight, up_mask, down_weight, down_mask, grad_out):
    share, width = tokens.shape
    total = share * lax.axis_size("col")
    part = total // CHUNKS // 8
    piece = share // CHUNKS
    blocks = width // BLOCK
    c = CHUNKS
    hbm = pl.BlockSpec(memory_space=pl.ANY)
    vmem = pl.BlockSpec(memory_space=pltpu.VMEM)
    return pl.pallas_call(
        kernel,
        out_shape=(
            jax.ShapeDtypeStruct((width // HEAD_DIM, share, HEAD_DIM), BF16),
            jax.ShapeDtypeStruct((share, width), BF16),
            jax.ShapeDtypeStruct(up_weight.shape, BF16),
            jax.ShapeDtypeStruct(down_weight.shape, BF16),
        ),
        in_specs=[hbm, hbm, vmem, hbm, vmem, hbm],
        out_specs=(vmem, vmem, hbm, hbm),
        scratch_shapes=[
            pltpu.VMEM((total, 2 * width), BF16),
            pltpu.VMEM(up_weight.shape, BF16),
            pltpu.VMEM(down_weight.shape, BF16),
            pltpu.VMEM((blocks, width), F32),
            pltpu.VMEM((blocks, width), F32),
            pltpu.VMEM((c, 2, 4, part, width), BF16),
            pltpu.VMEM((c, 2, 4, part, width), BF16),
            pltpu.VMEM((c, 4, part, width), BF16),
            pltpu.VMEM((c, 3, 2, part, width), BF16),
            pltpu.VMEM((c, part, width), BF16),
            pltpu.VMEM((c, part, width), F32),
            pltpu.VMEM((c, 3, part, width), BF16),
            pltpu.VMEM((c, part, width), BF16),
            pltpu.VMEM((c, 2, 4, part, width), BF16),
            pltpu.VMEM((c, 2, 4, part, width), BF16),
            pltpu.VMEM((c, 2, 4, 2 * piece, 2 * width), BF16),
            pltpu.VMEM((c, 4, 2 * piece, 2 * width), BF16),
            pltpu.VMEM((c, 3, 2 * piece, 2 * width), BF16),
            pltpu.VMEM((c, 2, piece, 2 * width), BF16),
            pltpu.VMEM((c, piece, 2 * width), BF16),
            pltpu.SemaphoreType.DMA((c, MESSAGES)),
            pltpu.SemaphoreType.DMA((c, MESSAGES)),
            pltpu.SemaphoreType.DMA((2 * c + 4,)),
        ],
        compiler_params=pltpu.CompilerParams(
            collective_id=0, has_side_effects=True, vmem_limit_bytes=67043328
        ),
        name="layer",
    )(tokens, up_weight, up_mask, down_weight, down_mask, grad_out)


def solution(mesh):
    return jax.shard_map(
        body,
        mesh=mesh,
        in_specs=(
            P("col", "row"),
            P("row", "col"),
            P("row", "col"),
            P("col", "row"),
            P("col", "row"),
            P("col", "row"),
        ),
        out_specs=(P("row", "col", None), P("col", "row"), P("row", "col"), P("col", "row")),
        check_vma=False,
    )
```

```python
import functools
import math

import jax
import jax.numpy as jnp
from jax import lax
from jax.experimental import pallas as pl
from jax.experimental.pallas import tpu as pltpu
from jax.sharding import PartitionSpec as P

BLOCK = 64
HEAD_DIM = 128
CHUNKS = 4
TILE = 256
WIDE = 768
GRAD_WIDE = 768
MESH = pl.DeviceIdType.MESH
F32 = jnp.float32
BF16 = jnp.bfloat16

AG_XH, AG_Y, AG_CORE = (0, 5), (1, 6), (4, 9)
R_CORE, R_Y, R_XH = (10, 15), (11, 16), (14, 19)
A_X, A_Z, B_Z, B_X = 20, 21, 24, 27
C_X, C_Z, D_Z, D_X = 28, 29, 32, 35
MESSAGES = 36
FWD, BWD = 0, 1


def dot_nn(left, right):
    return jnp.dot(left, right, preferred_element_type=F32)


def dot_nt(left, right):
    return lax.dot_general(left, right, (((1,), (1,)), ((), ())), preferred_element_type=F32)


def tile_at(index, tile=TILE):
    return pl.ds(pl.multiple_of(index * tile, tile), tile)


def kernel(
    tok, wup, mup, wdn, mdn, cot,
    oh, gt, gu, gd,
    tall, call, tturn, hturn, wu, wd, m2u, m2d, pa, pb, ra, rb, sb, sbo, r3a, r3b, hid, gra,
    outf, outb, r7f, r7b, ryf, ryb, s8f, s8b, rxf, rxb,
    ss, rs, ls,
):
    width = tok.shape[1]
    tokens = tall.shape[0]
    chunk = tokens // CHUNKS
    piece = tok.shape[0] // CHUNKS
    tiles = width // TILE
    grad_scale = 1.0 / math.sqrt(tokens)
    every = (tall, call)
    out, r_core, r_y, s_x, r_x = (outf, outb), (r7f, r7b), (ryf, ryb), (s8f, s8b), (rxf, rxb)

    row, col = lax.axis_index("row"), lax.axis_index("col")
    xl, z = row // 4, row % 4
    y, xh, k = col // 4, (col // 2) % 2, col % 2

    def device(xl=xl, z=z, y=y, xh=xh, k=k):
        return (xl * 4 + z, y * 4 + xh * 2 + k)

    z_to = [(z + d) % 4 for d in (1, 2, 3)]
    z_from = [(z + 4 - d) % 4 for d in (1, 2, 3)]
    y_to = [(y + d) % 4 for d in (1, 2, 3)]
    y_from = [(y + 4 - d) % 4 for d in (1, 2, 3)]
    x_dev, xh_dev, core_dev = device(xl=1 - xl), device(xh=1 - xh), device(k=1 - k)
    z_dev = [device(z=v) for v in z_to]
    y_dev = [device(y=v) for v in y_to]

    def rows_of(j, k_, y_, xh_, pieces):
        at = j * chunk + k_ * (chunk // 2) + y_ * (2 * piece) + xh_ * piece
        return pl.ds(pl.multiple_of(at, piece), pieces * piece)

    pending = []

    def send(j, i, src, dst, dev):
        copy = pltpu.make_async_remote_copy(
            src_ref=src, dst_ref=dst, send_sem=ss.at[j, i], recv_sem=rs.at[j, i],
            device_id=dev, device_id_type=MESH,
        )
        copy.start()
        pending.append(copy)

    def arrived(j, i, here, dev):
        pltpu.make_async_remote_copy(
            src_ref=here, dst_ref=here, send_sem=ss.at[j, i], recv_sem=rs.at[j, i],
            device_id=dev, device_id_type=MESH,
        ).wait_recv()

    own = {}
    for j in range(CHUNKS):
        for s, source in ((BWD, cot), (FWD, tok)):
            own[j, s] = pltpu.make_async_copy(
                source.at[pl.ds(j * piece, piece)], every[s].at[rows_of(j, k, y, xh, 1)], ls.at[2 * j + s]
            )
            own[j, s].start()
    load_dn = pltpu.make_async_copy(wdn, wd, ls.at[2 * CHUNKS])
    load_up = pltpu.make_async_copy(wup, wu, ls.at[2 * CHUNKS + 1])
    load_dn.start()
    load_up.start()

    barrier = pltpu.get_barrier_semaphore()
    for dev in [x_dev, xh_dev, core_dev] + z_dev + y_dev:
        pl.semaphore_signal(barrier, inc=1, device_id=dev, device_id_type=MESH)
    pl.semaphore_wait(barrier, 9)

    def ag_x(j, s):
        own[j, s].wait()
        at = every[s].at[rows_of(j, k, y, xh, 1)]
        send(j, AG_XH[s], at, at, xh_dev)

    def ag_y(j, s):
        arrived(j, AG_XH[s], every[s].at[rows_of(j, k, y, 1 - xh, 1)], xh_dev)
        at = every[s].at[rows_of(j, k, y, 0, 2)]
        for d in range(3):
            send(j, AG_Y[s] + d, at, at, y_dev[d])

    def ag_core(j, s):
        for d in range(3):
            arrived(j, AG_Y[s] + d, every[s].at[rows_of(j, k, y_from[d], 0, 2)], y_dev[d])
        at = every[s].at[rows_of(j, k, 0, 0, 8)]
        send(j, AG_CORE[s], at, at, core_dev)

    def up(j, s):
        arrived(j, AG_CORE[s], every[s].at[rows_of(j, 1 - k, 0, 0, 8)], core_dev)
        rows = pl.ds(j * chunk, chunk)

        @pl.loop(0, width // WIDE)
        def _(n):
            if s == FWD:
                value, place = dot_nn(tall[rows, :], wu[:, tile_at(n, WIDE)]), pa
            else:
                value, place = dot_nt(call[rows, :], wd[tile_at(n, WIDE), :]), pb
            place[j, :, :, :, tile_at(n, WIDE)] = value.astype(BF16).reshape(2, 4, chunk // 8, WIDE)

        if s == FWD:
            send(j, A_X, pa.at[j, 1 - xl], ra.at[j], x_dev)
        else:
            for d in range(3):
                send(j, A_Z + d, pb.at[j, :, z_to[d]], rb.at[j, d], z_dev[d])

    def sum_a(j):
        arrived(j, A_X, ra.at[j], x_dev)

        @pl.loop(0, 4)
        def _(v):
            pa[j, xl, v] = (pa[j, xl, v].astype(F32) + ra[j, v].astype(F32)).astype(BF16)

        for d in range(3):
            send(j, B_Z + d, pa.at[j, xl, z_to[d]], r3a.at[j, d], z_dev[d])
        for d in range(3):
            arrived(j, A_Z + d, rb.at[j, d], z_dev[d])

        def total(v):
            value = pb[j, v, z].astype(F32)
            for d in range(3):
                value = value + rb[j, d, v].astype(F32)
            return value

        sb[j] = total(1 - xl).astype(BF16)
        send(j, B_X, sb.at[j], r3b.at[j], x_dev)
        sbo[j] = total(xl)

    def sum_b(j):
        for d in range(3):
            arrived(j, B_Z + d, r3a.at[j, d], z_dev[d])
        arrived(j, B_X, r3b.at[j], x_dev)
        pre = pa[j, xl, z].astype(F32)
        for d in range(3):
            pre = pre + r3a[j, d].astype(F32)
        back = sbo[j] + r3b[j].astype(F32)
        root = 0.7978845608028654
        square = pre * pre
        bend = jnp.tanh(root * (pre + 0.044715 * (square * pre)))
        half = 0.5 * (1.0 + bend)
        slope = half + 0.5 * pre * (1.0 - bend * bend) * (root * (1.0 + 3 * 0.044715 * square))
        hid[j, xl, z] = (pre * half).astype(BF16)
        gra[j, xl, z] = (back * slope).astype(BF16)
        for d in range(3):
            send(j, C_Z + d, gra.at[j, xl, z], gra.at[j, xl, z], z_dev[d])
        send(j, C_X, hid.at[j, xl, z], hid.at[j, xl, z], x_dev)

    def spread(j):
        arrived(j, C_X, hid.at[j, 1 - xl, z], x_dev)
        for d in range(3):
            send(j, D_Z + d, hid.at[j, :, z], hid.at[j, :, z], z_dev[d])
        for d in range(3):
            arrived(j, C_Z + d, gra.at[j, xl, z_from[d]], z_dev[d])
        send(j, D_X, gra.at[j, xl], gra.at[j, xl], x_dev)

    def down(j, s):
        if s == FWD:
            for d in range(3):
                arrived(j, D_Z + d, hid.at[j, :, z_from[d]], z_dev[d])
        else:
            arrived(j, D_X, gra.at[j, 1 - xl], x_dev)

        @pl.loop(0, width // WIDE)
        def _(n):
            if s == FWD:
                value = dot_nn(hid[j].reshape(chunk, width), wd[:, tile_at(n, WIDE)])
            else:
                value = dot_nt(gra[j].reshape(chunk, width), wu[tile_at(n, WIDE), :])
            out[s][j, :, :, :, tile_at(n, WIDE)] = value.astype(BF16).reshape(2, 4, 2 * piece, WIDE)

        send(j, R_CORE[s], out[s].at[j, 1 - k], r_core[s].at[j], core_dev)

    def rs_core(j, s):
        arrived(j, R_CORE[s], r_core[s].at[j], core_dev)

        @pl.loop(0, 4)
        def _(v):
            out[s][j, k, v] = (out[s][j, k, v].astype(F32) + r_core[s][j, v].astype(F32)).astype(BF16)

        for d in range(3):
            send(j, R_Y[s] + d, out[s].at[j, k, y_to[d]], r_y[s].at[j, d], y_dev[d])

    def rs_y(j, s):
        for d in range(3):
            arrived(j, R_Y[s] + d, r_y[s].at[j, d], y_dev[d])
        value = out[s][j, k, y].astype(F32)
        for d in range(3):
            value = value + r_y[s][j, d].astype(F32)
        s_x[s][j] = value.astype(BF16).reshape(2, piece, width)
        send(j, R_XH[s], s_x[s].at[j, 1 - xh], r_x[s].at[j], xh_dev)

    def rs_x(j, s):
        arrived(j, R_XH[s], r_x[s].at[j], xh_dev)
        value = (s_x[s][j, xh].astype(F32) + r_x[s][j].astype(F32)).astype(BF16)
        here = pl.ds(j * piece, piece)
        if s == FWD:
            for head in range(width // HEAD_DIM):
                oh[head, here, :] = value[:, head * HEAD_DIM:(head + 1) * HEAD_DIM]
        else:
            gt[here, :] = value

    def turn(j, s):
        at = pl.ds(j * chunk, chunk)

        @pl.loop(0, tiles)
        def _(n):
            if s == FWD:
                hturn[tile_at(n), at] = hid[j, :, :, :, tile_at(n)].reshape(chunk, TILE).T
            else:
                tturn[tile_at(n), at] = tall[at, tile_at(n)].T

    stores = []

    def grad_slices(s, first, last):
        left, right, mask, place, result = (
            (hturn, call, m2d, wd, gd) if s == FWD else (tturn, gra, m2u, wu, gu)
        )

        def load(ref, t):
            if ref is gra:
                return ref[:, :, :, :, t].reshape(tokens, GRAD_WIDE)
            return ref[:, t]

        @pl.loop(first, last)
        def _(m):
            @pl.loop(0, width // GRAD_WIDE)
            def _(n):
                value = dot_nn(left[tile_at(m), :], load(right, tile_at(n, GRAD_WIDE))) * grad_scale
                for b in range(TILE // BLOCK):
                    keep = mask[pl.ds(m * (TILE // BLOCK) + b, 1), tile_at(n, GRAD_WIDE)]
                    part = value[b * BLOCK:(b + 1) * BLOCK] * keep
                    at = pl.ds(pl.multiple_of(m * TILE + b * BLOCK, BLOCK), BLOCK)
                    place[at, tile_at(n, GRAD_WIDE)] = part.astype(BF16)

        rows = pl.ds(first * TILE, (last - first) * TILE)
        copy = pltpu.make_async_copy(place.at[rows], result.at[rows], ls.at[2 * CHUNKS + 2 + len(stores)])
        copy.start()
        stores.append(copy)

    def keep_weights(mask, wide, weight, load):
        blocks = width // BLOCK
        at = lax.broadcasted_iota(jnp.int32, (blocks, width), 1)
        first = lax.broadcasted_iota(jnp.int32, (blocks, width), 0) * BLOCK
        repeat = jnp.where((at >= first) & (at < first + BLOCK), 1.0, 0.0).astype(F32)
        wide[...] = dot_nn(mask[...].astype(F32), repeat)
        load.wait()

        @pl.loop(0, blocks)
        def _(b):
            rows = pl.ds(pl.multiple_of(b * BLOCK, BLOCK), BLOCK)
            weight[rows, :] = weight[rows, :] * wide[pl.ds(b, 1), :].astype(BF16)

    both = (BWD, FWD)
    for j in range(CHUNKS):
        for s in both:
            ag_x(j, s)
    for s in both:
        ag_y(0, s)
    keep_weights(mdn, m2d, wd, load_dn)
    for s in both:
        ag_y(1, s)
    keep_weights(mup, m2u, wu, load_up)
    for j in (2, 3):
        for s in both:
            ag_y(j, s)

    def enter(j):
        for s in both:
            ag_core(j, s)
            up(j, s)

    def leave(step, j):
        for s in (FWD, BWD):
            step(j, s)

    enter(0)
    enter(1)
    sum_a(0)
    enter(2)
    sum_a(1)
    turn(0, BWD)
    sum_b(0)
    enter(3)
    turn(1, BWD)
    sum_b(1)
    spread(0)
    turn(2, BWD)
    sum_a(2)
    spread(1)
    sum_a(3)
    turn(3, BWD)
    leave(down, 0)
    sum_b(2)
    leave(rs_core, 0)
    leave(down, 1)
    sum_b(3)
    leave(rs_core, 1)
    turn(0, FWD)
    spread(2)
    turn(1, FWD)
    spread(3)
    leave(rs_y, 0)
    leave(rs_x, 0)
    leave(rs_y, 1)
    down(2, FWD)
    down(2, BWD)
    turn(2, FWD)
    leave(rs_core, 2)
    leave(rs_x, 1)
    down(3, FWD)
    down(3, BWD)
    rs_core(3, FWD)
    turn(3, FWD)
    rs_core(3, BWD)
    grad_slices(FWD, 0, 3)
    leave(rs_y, 2)
    grad_slices(FWD, 3, 6)
    rs_y(3, FWD)
    grad_slices(BWD, 0, 3)
    rs_y(3, BWD)
    grad_slices(BWD, 3, 6)
    leave(rs_x, 2)
    leave(rs_x, 3)
    for copy in pending:
        copy.wait_send()
    for copy in stores:
        copy.wait()


def hand_over(*refs):
    sources, results, held, sems = refs[:4], refs[4:8], refs[8:12], refs[12]
    moves = []
    for source, result, place in zip(sources, results, held):
        count = place.shape[0] // TILE if place.shape[0] > TILE else 1
        step = place.shape[0] // count
        for n in range(count):
            at = pl.ds(n * step, step)
            i = len(moves)
            moves.append((
                pltpu.make_async_copy(source.at[at], place.at[at], sems.at[0, i]),
                pltpu.make_async_copy(place.at[at], result.at[at], sems.at[1, i]),
            ))
    for first, _ in moves:
        first.start()
    for first, second in moves:
        first.wait()
        second.start()
    for _, second in moves:
        second.wait()


def body(tokens, up_weight, up_mask, down_weight, down_mask, grad_out):
    share, width = tokens.shape
    total = share * lax.axis_size("col")
    part = total // CHUNKS // 8
    piece = share // CHUNKS
    blocks = width // BLOCK
    c = CHUNKS
    hbm = pl.BlockSpec(memory_space=pl.ANY)
    vmem = pl.BlockSpec(memory_space=pltpu.VMEM)
    results = (
        jax.ShapeDtypeStruct((width // HEAD_DIM, share, HEAD_DIM), BF16),
        jax.ShapeDtypeStruct((share, width), BF16),
        jax.ShapeDtypeStruct(up_weight.shape, BF16),
        jax.ShapeDtypeStruct(down_weight.shape, BF16),
    )
    made = pl.pallas_call(
        kernel,
        out_shape=results,
        in_specs=[hbm, hbm, vmem, hbm, vmem, hbm],
        out_specs=(vmem, vmem, hbm, hbm),
        scratch_shapes=[
            pltpu.VMEM((total, width), BF16),
            pltpu.VMEM((total, width), BF16),
            pltpu.VMEM((width, total), BF16),
            pltpu.VMEM((width, total), BF16),
            pltpu.VMEM(up_weight.shape, BF16),
            pltpu.VMEM(down_weight.shape, BF16),
            pltpu.VMEM((blocks, width), F32),
            pltpu.VMEM((blocks, width), F32),
            pltpu.VMEM((c, 2, 4, part, width), BF16),
            pltpu.VMEM((c, 2, 4, part, width), BF16),
            pltpu.VMEM((c, 4, part, width), BF16),
            pltpu.VMEM((c, 3, 2, part, width), BF16),
            pltpu.VMEM((c, part, width), BF16),
            pltpu.VMEM((c, part, width), F32),
            pltpu.VMEM((c, 3, part, width), BF16),
            pltpu.VMEM((c, part, width), BF16),
            pltpu.VMEM((c, 2, 4, part, width), BF16),
            pltpu.VMEM((c, 2, 4, part, width), BF16),
            pltpu.VMEM((c, 2, 4, 2 * piece, width), BF16),
            pltpu.VMEM((c, 2, 4, 2 * piece, width), BF16),
            pltpu.VMEM((c, 4, 2 * piece, width), BF16),
            pltpu.VMEM((c, 4, 2 * piece, width), BF16),
            pltpu.VMEM((c, 3, 2 * piece, width), BF16),
            pltpu.VMEM((c, 3, 2 * piece, width), BF16),
            pltpu.VMEM((c, 2, piece, width), BF16),
            pltpu.VMEM((c, 2, piece, width), BF16),
            pltpu.VMEM((c, piece, width), BF16),
            pltpu.VMEM((c, piece, width), BF16),
            pltpu.SemaphoreType.DMA((c, MESSAGES)),
            pltpu.SemaphoreType.DMA((c, MESSAGES)),
            pltpu.SemaphoreType.DMA((2 * c + 8,)),
        ],
        compiler_params=pltpu.CompilerParams(
            collective_id=0, has_side_effects=True, vmem_limit_bytes=67043328
        ),
        name="layer",
    )(tokens, up_weight, up_mask, down_weight, down_mask, grad_out)
    return tuple(
        pl.pallas_call(
            hand_over,
            out_shape=results,
            in_specs=[hbm] * 4,
            out_specs=(hbm,) * 4,
            scratch_shapes=[pltpu.VMEM(r.shape, BF16) for r in results]
            + [pltpu.SemaphoreType.DMA((2, 16))],
            compiler_params=pltpu.CompilerParams(vmem_limit_bytes=67043328),
            name="hand_over",
        )(*made)
    )


def solution(mesh):
    return jax.shard_map(
        body,
        mesh=mesh,
        in_specs=(
            P("col", "row"),
            P("row", "col"),
            P("row", "col"),
            P("col", "row"),
            P("col", "row"),
            P("col", "row"),
        ),
        out_specs=(P("row", "col", None), P("col", "row"), P("row", "col"), P("col", "row")),
        check_vma=False,
    )
```

```python
import functools
import math

import jax
import jax.numpy as jnp
from jax import lax
from jax.experimental import pallas as pl
from jax.experimental.pallas import tpu as pltpu
from jax.sharding import PartitionSpec as P

BLOCK = 64
HEAD_DIM = 128
CHUNKS = 4
TILE = 256
WIDE = 768
GRAD_WIDE = 768
MESH = pl.DeviceIdType.MESH
F32 = jnp.float32
BF16 = jnp.bfloat16

AG_XH, AG_Y, AG_CORE = (0, 5), (1, 6), (4, 9)
R_CORE, R_Y, R_XH = (10, 15), (11, 16), (14, 19)
A_X, A_Z, B_Z, B_X = 20, 21, 24, 27
C_X, C_Z, D_Z, D_X = 28, 29, 32, 35
AG_Y2 = (36, 39)
MESSAGES = 42
FWD, BWD = 0, 1


def dot_nn(left, right):
    return jnp.dot(left, right, preferred_element_type=F32)


def dot_nt(left, right):
    return lax.dot_general(left, right, (((1,), (1,)), ((), ())), preferred_element_type=F32)


def tile_at(index, tile=TILE):
    return pl.ds(pl.multiple_of(index * tile, tile), tile)


def kernel(
    tok, wup, mup, wdn, mdn, cot,
    oh, gt, gu, gd,
    tall, call, tturn, hturn, wu, wd, m2u, m2d, pa, pb, ra, rb, sb, sbo, r3a, r3b, hid, gra,
    r7f, r7b, ryf, ryb, s8f, s8b, rxf, rxb,
    ss, rs, ls,
):
    width = tok.shape[1]
    tokens = tall.shape[0]
    chunk = tokens // CHUNKS
    piece = tok.shape[0] // CHUNKS
    tiles = width // TILE
    grad_scale = 1.0 / math.sqrt(tokens)
    every = (tall, call)
    out, r_core, r_y, s_x, r_x = (pa, pb), (r7f, r7b), (ryf, ryb), (s8f, s8b), (rxf, rxb)

    row, col = lax.axis_index("row"), lax.axis_index("col")
    xl, z = row // 4, row % 4
    y, xh, k = col // 4, (col // 2) % 2, col % 2

    def device(xl=xl, z=z, y=y, xh=xh, k=k):
        return (xl * 4 + z, y * 4 + xh * 2 + k)

    z_to = [(z + d) % 4 for d in (1, 2, 3)]
    z_from = [(z + 4 - d) % 4 for d in (1, 2, 3)]
    y_to = [(y + d) % 4 for d in (1, 2, 3)]
    y_from = [(y + 4 - d) % 4 for d in (1, 2, 3)]
    x_dev, xh_dev, core_dev = device(xl=1 - xl), device(xh=1 - xh), device(k=1 - k)
    z_dev = [device(z=v) for v in z_to]
    y_dev = [device(y=v) for v in y_to]

    def rows_of(j, k_, y_, xh_, pieces):
        at = j * chunk + k_ * (chunk // 2) + y_ * (2 * piece) + xh_ * piece
        return pl.ds(pl.multiple_of(at, piece), pieces * piece)

    pending = {}

    def send(j, i, src, dst, dev):
        copy = pltpu.make_async_remote_copy(
            src_ref=src, dst_ref=dst, send_sem=ss.at[j, i], recv_sem=rs.at[j, i],
            device_id=dev, device_id_type=MESH,
        )
        copy.start()
        pending[j, i] = copy

    def arrived(j, i, here, dev):
        pltpu.make_async_remote_copy(
            src_ref=here, dst_ref=here, send_sem=ss.at[j, i], recv_sem=rs.at[j, i],
            device_id=dev, device_id_type=MESH,
        ).wait_recv()

    own = {}
    for j in range(CHUNKS):
        for s, source in ((BWD, cot), (FWD, tok)):
            own[j, s] = pltpu.make_async_copy(
                source.at[pl.ds(j * piece, piece)], every[s].at[rows_of(j, k, y, xh, 1)], ls.at[2 * j + s]
            )
            own[j, s].start()
    load_dn = pltpu.make_async_copy(wdn, wd, ls.at[2 * CHUNKS])
    load_up = pltpu.make_async_copy(wup, wu, ls.at[2 * CHUNKS + 1])
    load_dn.start()
    load_up.start()

    barrier = pltpu.get_barrier_semaphore()
    for dev in [x_dev, xh_dev, core_dev] + z_dev + y_dev:
        pl.semaphore_signal(barrier, inc=1, device_id=dev, device_id_type=MESH)
    pl.semaphore_wait(barrier, 9)

    def ag_x(j, s):
        own[j, s].wait()
        at = every[s].at[rows_of(j, k, y, xh, 1)]
        send(j, AG_XH[s], at, at, xh_dev)

    def ag_own(j, s):
        at = every[s].at[rows_of(j, k, y, xh, 1)]
        for d in range(3):
            send(j, AG_Y[s] + d, at, at, y_dev[d])

    def ag_y(j, s):
        at = every[s].at[rows_of(j, k, y, 1 - xh, 1)]
        arrived(j, AG_XH[s], at, xh_dev)
        for d in range(3):
            send(j, AG_Y2[s] + d, at, at, y_dev[d])

    def ag_core(j, s):
        for d in range(3):
            arrived(j, AG_Y[s] + d, every[s].at[rows_of(j, k, y_from[d], xh, 1)], y_dev[d])
        for d in range(3):
            arrived(j, AG_Y2[s] + d, every[s].at[rows_of(j, k, y_from[d], 1 - xh, 1)], y_dev[d])
        at = every[s].at[rows_of(j, k, 0, 0, 8)]
        send(j, AG_CORE[s], at, at, core_dev)

    def up(j, s):
        arrived(j, AG_CORE[s], every[s].at[rows_of(j, 1 - k, 0, 0, 8)], core_dev)
        rows = pl.ds(j * chunk, chunk)

        @pl.loop(0, width // WIDE)
        def _(n):
            if s == FWD:
                value, place = dot_nn(tall[rows, :], wu[:, tile_at(n, WIDE)]), pa
            else:
                value, place = dot_nt(call[rows, :], wd[tile_at(n, WIDE), :]), pb
            place[j, :, :, :, tile_at(n, WIDE)] = value.astype(BF16).reshape(2, 4, chunk // 8, WIDE)

        if s == FWD:
            send(j, A_X, pa.at[j, 1 - xl], ra.at[j], x_dev)
        else:
            for d in range(3):
                send(j, A_Z + d, pb.at[j, :, z_to[d]], rb.at[j, d], z_dev[d])

    def sum_a(j):
        arrived(j, A_X, ra.at[j], x_dev)

        @pl.loop(0, 4)
        def _(v):
            pa[j, xl, v] = (pa[j, xl, v].astype(F32) + ra[j, v].astype(F32)).astype(BF16)

        for d in range(3):
            send(j, B_Z + d, pa.at[j, xl, z_to[d]], r3a.at[j, d], z_dev[d])
        for d in range(3):
            arrived(j, A_Z + d, rb.at[j, d], z_dev[d])

        def total(v):
            value = pb[j, v, z].astype(F32)
            for d in range(3):
                value = value + rb[j, d, v].astype(F32)
            return value

        sb[j] = total(1 - xl).astype(BF16)
        send(j, B_X, sb.at[j], r3b.at[j], x_dev)
        sbo[j] = total(xl)

    def sum_b(j):
        for d in range(3):
            arrived(j, B_Z + d, r3a.at[j, d], z_dev[d])
        arrived(j, B_X, r3b.at[j], x_dev)
        pre = pa[j, xl, z].astype(F32)
        for d in range(3):
            pre = pre + r3a[j, d].astype(F32)
        back = sbo[j] + r3b[j].astype(F32)
        root = 0.7978845608028654
        square = pre * pre
        bend = jnp.tanh(root * (pre + 0.044715 * (square * pre)))
        half = 0.5 * (1.0 + bend)
        slope = half + 0.5 * pre * (1.0 - bend * bend) * (root * (1.0 + 3 * 0.044715 * square))
        hid[j, xl, z] = (pre * half).astype(BF16)
        gra[j, xl, z] = (back * slope).astype(BF16)
        for d in range(3):
            send(j, C_Z + d, gra.at[j, xl, z], gra.at[j, xl, z], z_dev[d])
        send(j, C_X, hid.at[j, xl, z], hid.at[j, xl, z], x_dev)

    def spread(j):
        arrived(j, C_X, hid.at[j, 1 - xl, z], x_dev)
        for d in range(3):
            send(j, D_Z + d, hid.at[j, :, z], hid.at[j, :, z], z_dev[d])
        for d in range(3):
            arrived(j, C_Z + d, gra.at[j, xl, z_from[d]], z_dev[d])
        send(j, D_X, gra.at[j, xl], gra.at[j, xl], x_dev)

    def down(j, s):
        if s == FWD:
            for d in range(3):
                arrived(j, D_Z + d, hid.at[j, :, z_from[d]], z_dev[d])
        else:
            arrived(j, D_X, gra.at[j, 1 - xl], x_dev)
        for i in (A_X, B_Z, B_Z + 1, B_Z + 2) if s == FWD else (A_Z, A_Z + 1, A_Z + 2):
            pending.pop((j, i)).wait_send()

        @pl.loop(0, width // WIDE)
        def _(n):
            if s == FWD:
                value = dot_nn(hid[j].reshape(chunk, width), wd[:, tile_at(n, WIDE)])
            else:
                value = dot_nt(gra[j].reshape(chunk, width), wu[tile_at(n, WIDE), :])
            out[s][j, :, :, :, tile_at(n, WIDE)] = value.astype(BF16).reshape(2, 4, 2 * piece, WIDE)

        send(j, R_CORE[s], out[s].at[j, 1 - k], r_core[s].at[j], core_dev)

    def rs_core(j, s):
        arrived(j, R_CORE[s], r_core[s].at[j], core_dev)

        @pl.loop(0, 4)
        def _(v):
            out[s][j, k, v] = (out[s][j, k, v].astype(F32) + r_core[s][j, v].astype(F32)).astype(BF16)

        for d in range(3):
            send(j, R_Y[s] + d, out[s].at[j, k, y_to[d]], r_y[s].at[j, d], y_dev[d])

    def rs_y(j, s):
        for d in range(3):
            arrived(j, R_Y[s] + d, r_y[s].at[j, d], y_dev[d])
        value = out[s][j, k, y].astype(F32)
        for d in range(3):
            value = value + r_y[s][j, d].astype(F32)
        s_x[s][j] = value.astype(BF16).reshape(2, piece, width)
        send(j, R_XH[s], s_x[s].at[j, 1 - xh], r_x[s].at[j], xh_dev)

    def rs_x(j, s):
        arrived(j, R_XH[s], r_x[s].at[j], xh_dev)
        value = (s_x[s][j, xh].astype(F32) + r_x[s][j].astype(F32)).astype(BF16)
        here = pl.ds(j * piece, piece)
        if s == FWD:
            for head in range(width // HEAD_DIM):
                oh[head, here, :] = value[:, head * HEAD_DIM:(head + 1) * HEAD_DIM]
        else:
            gt[here, :] = value

    def turn(j, s):
        at = pl.ds(j * chunk, chunk)

        @pl.loop(0, tiles)
        def _(n):
            if s == FWD:
                hturn[tile_at(n), at] = hid[j, :, :, :, tile_at(n)].reshape(chunk, TILE).T
            else:
                tturn[tile_at(n), at] = tall[at, tile_at(n)].T


    def grad_slices(s, first, last):
        left, right, mask, place = (
            (hturn, call, m2d, gd) if s == FWD else (tturn, gra, m2u, gu)
        )

        def load(ref, t):
            if ref is gra:
                return ref[:, :, :, :, t].reshape(tokens, GRAD_WIDE)
            return ref[:, t]

        @pl.loop(first, last)
        def _(m):
            @pl.loop(0, width // GRAD_WIDE)
            def _(n):
                value = dot_nn(left[tile_at(m), :], load(right, tile_at(n, GRAD_WIDE))) * grad_scale
                for b in range(TILE // BLOCK):
                    keep = mask[pl.ds(m * (TILE // BLOCK) + b, 1), tile_at(n, GRAD_WIDE)]
                    part = value[b * BLOCK:(b + 1) * BLOCK] * keep
                    at = pl.ds(pl.multiple_of(m * TILE + b * BLOCK, BLOCK), BLOCK)
                    place[at, tile_at(n, GRAD_WIDE)] = part.astype(BF16)


    def keep_weights(mask, wide, weight, load):
        blocks = width // BLOCK
        at = lax.broadcasted_iota(jnp.int32, (blocks, width), 1)
        first = lax.broadcasted_iota(jnp.int32, (blocks, width), 0) * BLOCK
        repeat = jnp.where((at >= first) & (at < first + BLOCK), 1.0, 0.0).astype(F32)
        wide[...] = dot_nn(mask[...].astype(F32), repeat)
        load.wait()

        @pl.loop(0, blocks)
        def _(b):
            rows = pl.ds(pl.multiple_of(b * BLOCK, BLOCK), BLOCK)
            weight[rows, :] = weight[rows, :] * wide[pl.ds(b, 1), :].astype(BF16)

    both = (BWD, FWD)
    for s in both:
        ag_x(0, s)
        ag_own(0, s)
    for j in range(1, CHUNKS):
        for s in both:
            ag_x(j, s)
    for s in both:
        ag_y(0, s)
    keep_weights(mdn, m2d, wd, load_dn)
    for s in both:
        ag_own(1, s)
        ag_y(1, s)
    keep_weights(mup, m2u, wu, load_up)
    for j in (2, 3):
        for s in both:
            ag_own(j, s)
            ag_y(j, s)

    def enter(j):
        for s in both:
            ag_core(j, s)
            up(j, s)

    def leave(step, j):
        for s in (FWD, BWD):
            step(j, s)

    enter(0)
    enter(1)
    sum_a(0)
    enter(2)
    sum_a(1)
    turn(0, BWD)
    sum_b(0)
    enter(3)
    turn(1, BWD)
    sum_b(1)
    spread(0)
    turn(2, BWD)
    sum_a(2)
    spread(1)
    turn(3, BWD)
    leave(down, 0)
    sum_b(2)
    sum_a(3)
    leave(rs_core, 0)
    leave(down, 1)
    spread(2)
    leave(rs_core, 1)
    sum_b(3)
    turn(0, FWD)
    turn(1, FWD)
    leave(rs_y, 0)
    leave(rs_x, 0)
    spread(3)
    down(2, FWD)
    down(2, BWD)
    leave(rs_core, 2)
    turn(2, FWD)
    leave(rs_y, 1)
    leave(rs_x, 1)
    down(3, FWD)
    down(3, BWD)
    rs_core(3, FWD)
    turn(3, FWD)
    rs_core(3, BWD)
    grad_slices(FWD, 0, 3)
    leave(rs_y, 2)
    grad_slices(FWD, 3, 6)
    rs_y(3, FWD)
    grad_slices(BWD, 0, 2)
    rs_y(3, BWD)
    grad_slices(BWD, 2, 5)
    leave(rs_x, 2)
    leave(rs_x, 3)
    grad_slices(BWD, 5, 6)
    for copy in pending.values():
        copy.wait_send()


def hand_over(*refs):
    made, results, sems = refs[:4], refs[4:8], refs[8]
    copies = [
        pltpu.make_async_copy(source, result, sems.at[i])
        for i, (source, result) in enumerate(zip(made, results))
    ]
    for copy in copies:
        copy.start()
    for copy in copies:
        copy.wait()


def body(tokens, up_weight, up_mask, down_weight, down_mask, grad_out):
    share, width = tokens.shape
    total = share * lax.axis_size("col")
    part = total // CHUNKS // 8
    piece = share // CHUNKS
    blocks = width // BLOCK
    c = CHUNKS
    hbm = pl.BlockSpec(memory_space=pl.ANY)
    vmem = pl.BlockSpec(memory_space=pltpu.VMEM)
    results = (
        jax.ShapeDtypeStruct((width // HEAD_DIM, share, HEAD_DIM), BF16),
        jax.ShapeDtypeStruct((share, width), BF16),
        jax.ShapeDtypeStruct(up_weight.shape, BF16),
        jax.ShapeDtypeStruct(down_weight.shape, BF16),
    )
    made = pl.pallas_call(
        kernel,
        out_shape=tuple(pltpu.VMEM(r.shape, BF16) for r in results),
        in_specs=[hbm, hbm, vmem, hbm, vmem, hbm],
        out_specs=(vmem,) * 4,
        scratch_shapes=[
            pltpu.VMEM((total, width), BF16),
            pltpu.VMEM((total, width), BF16),
            pltpu.VMEM((width, total), BF16),
            pltpu.VMEM((width, total), BF16),
            pltpu.VMEM(up_weight.shape, BF16),
            pltpu.VMEM(down_weight.shape, BF16),
            pltpu.VMEM((blocks, width), F32),
            pltpu.VMEM((blocks, width), F32),
            pltpu.VMEM((c, 2, 4, part, width), BF16),
            pltpu.VMEM((c, 2, 4, part, width), BF16),
            pltpu.VMEM((c, 4, part, width), BF16),
            pltpu.VMEM((c, 3, 2, part, width), BF16),
            pltpu.VMEM((c, part, width), BF16),
            pltpu.VMEM((c, part, width), F32),
            pltpu.VMEM((c, 3, part, width), BF16),
            pltpu.VMEM((c, part, width), BF16),
            pltpu.VMEM((c, 2, 4, part, width), BF16),
            pltpu.VMEM((c, 2, 4, part, width), BF16),
            pltpu.VMEM((c, 4, 2 * piece, width), BF16),
            pltpu.VMEM((c, 4, 2 * piece, width), BF16),
            pltpu.VMEM((c, 3, 2 * piece, width), BF16),
            pltpu.VMEM((c, 3, 2 * piece, width), BF16),
            pltpu.VMEM((c, 2, piece, width), BF16),
            pltpu.VMEM((c, 2, piece, width), BF16),
            pltpu.VMEM((c, piece, width), BF16),
            pltpu.VMEM((c, piece, width), BF16),
            pltpu.SemaphoreType.DMA((c, MESSAGES)),
            pltpu.SemaphoreType.DMA((c, MESSAGES)),
            pltpu.SemaphoreType.DMA((2 * c + 2,)),
        ],
        compiler_params=pltpu.CompilerParams(
            collective_id=0, has_side_effects=True, vmem_limit_bytes=57000000
        ),
        name="layer",
    )(tokens, up_weight, up_mask, down_weight, down_mask, grad_out)
    return tuple(
        pl.pallas_call(
            hand_over,
            out_shape=results,
            in_specs=[vmem] * 4,
            out_specs=(hbm,) * 4,
            scratch_shapes=[pltpu.SemaphoreType.DMA((4,))],
            compiler_params=pltpu.CompilerParams(vmem_limit_bytes=1 << 20),
            name="hand_over",
        )(*made)
    )


def solution(mesh):
    return jax.shard_map(
        body,
        mesh=mesh,
        in_specs=(
            P("col", "row"),
            P("row", "col"),
            P("row", "col"),
            P("col", "row"),
            P("col", "row"),
            P("col", "row"),
        ),
        out_specs=(P("row", "col", None), P("col", "row"), P("row", "col"), P("col", "row")),
        check_vma=False,
    )
```

```python
import functools
import math

import jax
import jax.numpy as jnp
from jax import lax
from jax.experimental import pallas as pl
from jax.experimental.pallas import tpu as pltpu
from jax.sharding import PartitionSpec as P

BLOCK = 64
HEAD_DIM = 128
CHUNKS = 4
TILE = 256
WIDE = 768
GRAD_WIDE = 768
MESH = pl.DeviceIdType.MESH
F32 = jnp.float32
BF16 = jnp.bfloat16

AG_XH, AG_Y, AG_CORE = (0, 5), (1, 6), (4, 9)
R_CORE, R_Y, R_XH = (10, 15), (11, 16), (14, 19)
A_X, A_Z, B_Z, B_X = 20, 21, 24, 27
C_X, C_Z, D_Z, D_X = 28, 29, 32, 35
AG_Y2 = (36, 39)
A_X2, A_Z2, R_CORE2 = 42, 43, (46, 47)
MESSAGES = 48
FWD, BWD = 0, 1


def dot_nn(left, right):
    return jnp.dot(left, right, preferred_element_type=F32)


def dot_nt(left, right):
    return lax.dot_general(left, right, (((1,), (1,)), ((), ())), preferred_element_type=F32)


def tile_at(index, tile=TILE):
    return pl.ds(pl.multiple_of(index * tile, tile), tile)


def kernel(
    tok, wup, mup, wdn, mdn, cot,
    oh, gt, gu, gd,
    tall, call, tturn, hturn, wu, wd, m2u, m2d, pa, pb, ra, rb, sb, sbo, r3a, r3b, hid, gra,
    r7f, r7b, ryf, ryb, s8f, s8b, rxf, rxb,
    ss, rs, ls,
):
    width = tok.shape[1]
    tokens = tall.shape[0]
    chunk = tokens // CHUNKS
    piece = tok.shape[0] // CHUNKS
    tiles = width // TILE
    grad_scale = 1.0 / math.sqrt(tokens)
    every = (tall, call)
    out, r_core, r_y, s_x, r_x = (pa, pb), (r7f, r7b), (ryf, ryb), (s8f, s8b), (rxf, rxb)

    row, col = lax.axis_index("row"), lax.axis_index("col")
    xl, z = row // 4, row % 4
    y, xh, k = col // 4, (col // 2) % 2, col % 2

    def device(xl=xl, z=z, y=y, xh=xh, k=k):
        return (xl * 4 + z, y * 4 + xh * 2 + k)

    z_to = [(z + d) % 4 for d in (1, 2, 3)]
    z_from = [(z + 4 - d) % 4 for d in (1, 2, 3)]
    y_to = [(y + d) % 4 for d in (1, 2, 3)]
    y_from = [(y + 4 - d) % 4 for d in (1, 2, 3)]
    x_dev, xh_dev, core_dev = device(xl=1 - xl), device(xh=1 - xh), device(k=1 - k)
    z_dev = [device(z=v) for v in z_to]
    y_dev = [device(y=v) for v in y_to]

    def rows_of(j, k_, y_, xh_, pieces):
        at = j * chunk + k_ * (chunk // 2) + y_ * (2 * piece) + xh_ * piece
        return pl.ds(pl.multiple_of(at, piece), pieces * piece)

    pending = {}

    def send(j, i, src, dst, dev):
        copy = pltpu.make_async_remote_copy(
            src_ref=src, dst_ref=dst, send_sem=ss.at[j, i], recv_sem=rs.at[j, i],
            device_id=dev, device_id_type=MESH,
        )
        copy.start()
        pending[j, i] = copy

    def arrived(j, i, here, dev):
        pltpu.make_async_remote_copy(
            src_ref=here, dst_ref=here, send_sem=ss.at[j, i], recv_sem=rs.at[j, i],
            device_id=dev, device_id_type=MESH,
        ).wait_recv()

    own = {}
    for j in range(CHUNKS):
        for s, source in ((BWD, cot), (FWD, tok)):
            own[j, s] = pltpu.make_async_copy(
                source.at[pl.ds(j * piece, piece)], every[s].at[rows_of(j, k, y, xh, 1)], ls.at[2 * j + s]
            )
            own[j, s].start()
    load_dn = pltpu.make_async_copy(wdn, wd, ls.at[2 * CHUNKS])
    load_up = pltpu.make_async_copy(wup, wu, ls.at[2 * CHUNKS + 1])
    load_dn.start()
    load_up.start()

    barrier = pltpu.get_barrier_semaphore()
    for dev in [x_dev, xh_dev, core_dev] + z_dev + y_dev:
        pl.semaphore_signal(barrier, inc=1, device_id=dev, device_id_type=MESH)
    pl.semaphore_wait(barrier, 9)

    def ag_x(j, s):
        own[j, s].wait()
        at = every[s].at[rows_of(j, k, y, xh, 1)]
        send(j, AG_XH[s], at, at, xh_dev)

    def ag_own(j, s):
        at = every[s].at[rows_of(j, k, y, xh, 1)]
        for d in range(3):
            send(j, AG_Y[s] + d, at, at, y_dev[d])

    def ag_y(j, s):
        at = every[s].at[rows_of(j, k, y, 1 - xh, 1)]
        arrived(j, AG_XH[s], at, xh_dev)
        for d in range(3):
            send(j, AG_Y2[s] + d, at, at, y_dev[d])

    def ag_core(j, s):
        for d in range(3):
            arrived(j, AG_Y[s] + d, every[s].at[rows_of(j, k, y_from[d], xh, 1)], y_dev[d])
        for d in range(3):
            arrived(j, AG_Y2[s] + d, every[s].at[rows_of(j, k, y_from[d], 1 - xh, 1)], y_dev[d])
        at = every[s].at[rows_of(j, k, 0, 0, 8)]
        send(j, AG_CORE[s], at, at, core_dev)

    def up(j, s):
        arrived(j, AG_CORE[s], every[s].at[rows_of(j, 1 - k, 0, 0, 8)], core_dev)
        rows = pl.ds(j * chunk, chunk)

        def product(at):
            if s == FWD:
                value, place = dot_nn(tall[rows, :], wu[:, at]), pa
            else:
                value, place = dot_nt(call[rows, :], wd[at, :]), pb
            place[j, :, :, :, at] = value.astype(BF16).reshape(2, 4, chunk // 8, WIDE)

        def leave_with(at, to_x, to_z):
            if s == FWD:
                send(j, to_x, pa.at[j, 1 - xl, :, :, at], ra.at[j, :, :, at], x_dev)
            else:
                for d in range(3):
                    send(j, to_z + d, pb.at[j, :, z_to[d], :, at], rb.at[j, d, :, :, at], z_dev[d])

        if j == 0:
            for n, (to_x, to_z) in enumerate(((A_X, A_Z), (A_X2, A_Z2))):
                product(pl.ds(n * WIDE, WIDE))
                leave_with(pl.ds(n * WIDE, WIDE), to_x, to_z)
        else:
            @pl.loop(0, width // WIDE)
            def _(n):
                product(tile_at(n, WIDE))

            leave_with(pl.ds(0, width), A_X, A_Z)

    def halves(j, at_chunk, first, second):
        if j == at_chunk:
            return [(first, pl.ds(0, WIDE)), (second, pl.ds(WIDE, WIDE))]
        return [(first, pl.ds(0, width))]

    def sum_a(j):
        for i, at in halves(j, 0, A_X, A_X2):
            arrived(j, i, ra.at[j, :, :, at], x_dev)

        @pl.loop(0, 4)
        def _(v):
            pa[j, xl, v] = (pa[j, xl, v].astype(F32) + ra[j, v].astype(F32)).astype(BF16)

        for d in range(3):
            send(j, B_Z + d, pa.at[j, xl, z_to[d]], r3a.at[j, d], z_dev[d])
        for d in range(3):
            for i, at in halves(j, 0, A_Z, A_Z2):
                arrived(j, i + d, rb.at[j, d, :, :, at], z_dev[d])

        def total(v):
            value = pb[j, v, z].astype(F32)
            for d in range(3):
                value = value + rb[j, d, v].astype(F32)
            return value

        sb[j] = total(1 - xl).astype(BF16)
        send(j, B_X, sb.at[j], r3b.at[j], x_dev)
        sbo[j] = total(xl)

    def sum_b(j):
        for d in range(3):
            arrived(j, B_Z + d, r3a.at[j, d], z_dev[d])
        arrived(j, B_X, r3b.at[j], x_dev)
        pre = pa[j, xl, z].astype(F32)
        for d in range(3):
            pre = pre + r3a[j, d].astype(F32)
        back = sbo[j] + r3b[j].astype(F32)
        root = 0.7978845608028654
        square = pre * pre
        bend = jnp.tanh(root * (pre + 0.044715 * (square * pre)))
        half = 0.5 * (1.0 + bend)
        slope = half + 0.5 * pre * (1.0 - bend * bend) * (root * (1.0 + 3 * 0.044715 * square))
        hid[j, xl, z] = (pre * half).astype(BF16)
        gra[j, xl, z] = (back * slope).astype(BF16)
        for d in range(3):
            send(j, C_Z + d, gra.at[j, xl, z], gra.at[j, xl, z], z_dev[d])
        send(j, C_X, hid.at[j, xl, z], hid.at[j, xl, z], x_dev)

    def spread(j):
        arrived(j, C_X, hid.at[j, 1 - xl, z], x_dev)
        for d in range(3):
            send(j, D_Z + d, hid.at[j, :, z], hid.at[j, :, z], z_dev[d])
        for d in range(3):
            arrived(j, C_Z + d, gra.at[j, xl, z_from[d]], z_dev[d])
        send(j, D_X, gra.at[j, xl], gra.at[j, xl], x_dev)

    def down(j, s):
        if s == FWD:
            for d in range(3):
                arrived(j, D_Z + d, hid.at[j, :, z_from[d]], z_dev[d])
        else:
            arrived(j, D_X, gra.at[j, 1 - xl], x_dev)
        for i in (A_X, A_X2, B_Z, B_Z + 1, B_Z + 2) if s == FWD else [
            first + d for first in (A_Z, A_Z2) for d in range(3)
        ]:
            if (j, i) in pending:
                pending.pop((j, i)).wait_send()

        def product(at):
            if s == FWD:
                value = dot_nn(hid[j].reshape(chunk, width), wd[:, at])
            else:
                value = dot_nt(gra[j].reshape(chunk, width), wu[at, :])
            out[s][j, :, :, :, at] = value.astype(BF16).reshape(2, 4, 2 * piece, WIDE)

        def leave_with(i, at):
            send(j, i, out[s].at[j, 1 - k, :, :, at], r_core[s].at[j, :, :, at], core_dev)

        if j == CHUNKS - 1:
            for i, at in halves(j, j, R_CORE[s], R_CORE2[s]):
                product(at)
                leave_with(i, at)
        else:
            @pl.loop(0, width // WIDE)
            def _(n):
                product(tile_at(n, WIDE))

            leave_with(R_CORE[s], pl.ds(0, width))

    def rs_core(j, s):
        for i, at in halves(j, CHUNKS - 1, R_CORE[s], R_CORE2[s]):
            arrived(j, i, r_core[s].at[j, :, :, at], core_dev)

        @pl.loop(0, 4)
        def _(v):
            out[s][j, k, v] = (out[s][j, k, v].astype(F32) + r_core[s][j, v].astype(F32)).astype(BF16)

        for d in range(3):
            send(j, R_Y[s] + d, out[s].at[j, k, y_to[d]], r_y[s].at[j, d], y_dev[d])

    def rs_y(j, s):
        for d in range(3):
            arrived(j, R_Y[s] + d, r_y[s].at[j, d], y_dev[d])
        value = out[s][j, k, y].astype(F32)
        for d in range(3):
            value = value + r_y[s][j, d].astype(F32)
        s_x[s][j] = value.astype(BF16).reshape(2, piece, width)
        send(j, R_XH[s], s_x[s].at[j, 1 - xh], r_x[s].at[j], xh_dev)

    def rs_x(j, s):
        arrived(j, R_XH[s], r_x[s].at[j], xh_dev)
        value = (s_x[s][j, xh].astype(F32) + r_x[s][j].astype(F32)).astype(BF16)
        here = pl.ds(j * piece, piece)
        if s == FWD:
            for head in range(width // HEAD_DIM):
                oh[head, here, :] = value[:, head * HEAD_DIM:(head + 1) * HEAD_DIM]
        else:
            gt[here, :] = value

    def turn(j, s):
        at = pl.ds(j * chunk, chunk)

        @pl.loop(0, tiles)
        def _(n):
            if s == FWD:
                hturn[tile_at(n), at] = hid[j, :, :, :, tile_at(n)].reshape(chunk, TILE).T
            else:
                tturn[tile_at(n), at] = tall[at, tile_at(n)].T


    def grad_slices(s, first, last):
        left, right, mask, place = (
            (hturn, call, m2d, gd) if s == FWD else (tturn, gra, m2u, gu)
        )

        def load(ref, t):
            if ref is gra:
                return ref[:, :, :, :, t].reshape(tokens, GRAD_WIDE)
            return ref[:, t]

        @pl.loop(first, last)
        def _(m):
            @pl.loop(0, width // GRAD_WIDE)
            def _(n):
                value = dot_nn(left[tile_at(m), :], load(right, tile_at(n, GRAD_WIDE))) * grad_scale
                for b in range(TILE // BLOCK):
                    keep = mask[pl.ds(m * (TILE // BLOCK) + b, 1), tile_at(n, GRAD_WIDE)]
                    part = value[b * BLOCK:(b + 1) * BLOCK] * keep
                    at = pl.ds(pl.multiple_of(m * TILE + b * BLOCK, BLOCK), BLOCK)
                    place[at, tile_at(n, GRAD_WIDE)] = part.astype(BF16)


    def keep_weights(mask, wide, weight, load):
        blocks = width // BLOCK
        at = lax.broadcasted_iota(jnp.int32, (blocks, width), 1)
        first = lax.broadcasted_iota(jnp.int32, (blocks, width), 0) * BLOCK
        repeat = jnp.where((at >= first) & (at < first + BLOCK), 1.0, 0.0).astype(F32)
        wide[...] = dot_nn(mask[...].astype(F32), repeat)
        load.wait()

        @pl.loop(0, blocks)
        def _(b):
            rows = pl.ds(pl.multiple_of(b * BLOCK, BLOCK), BLOCK)
            weight[rows, :] = weight[rows, :] * wide[pl.ds(b, 1), :].astype(BF16)

    both = (BWD, FWD)
    for s in both:
        ag_x(0, s)
        ag_own(0, s)
    for j in range(1, CHUNKS):
        for s in both:
            ag_x(j, s)
    for s in both:
        ag_y(0, s)
    keep_weights(mdn, m2d, wd, load_dn)
    for s in both:
        ag_own(1, s)
        ag_y(1, s)
    keep_weights(mup, m2u, wu, load_up)
    for j in (2, 3):
        for s in both:
            ag_own(j, s)
            ag_y(j, s)

    def enter(j):
        for s in both:
            ag_core(j, s)
            up(j, s)

    def leave(step, j):
        for s in (FWD, BWD):
            step(j, s)

    enter(0)
    enter(1)
    sum_a(0)
    enter(2)
    sum_a(1)
    turn(0, BWD)
    sum_b(0)
    enter(3)
    turn(1, BWD)
    sum_b(1)
    spread(0)
    turn(2, BWD)
    sum_a(2)
    spread(1)
    turn(3, BWD)
    leave(down, 0)
    sum_b(2)
    sum_a(3)
    leave(rs_core, 0)
    leave(down, 1)
    spread(2)
    leave(rs_core, 1)
    sum_b(3)
    turn(0, FWD)
    turn(1, FWD)
    leave(rs_y, 0)
    leave(rs_x, 0)
    spread(3)
    down(2, FWD)
    down(2, BWD)
    leave(rs_core, 2)
    turn(2, FWD)
    leave(rs_y, 1)
    leave(rs_x, 1)
    down(3, FWD)
    down(3, BWD)
    rs_core(3, FWD)
    turn(3, FWD)
    rs_core(3, BWD)
    grad_slices(FWD, 0, 3)
    leave(rs_y, 2)
    grad_slices(FWD, 3, 6)
    rs_y(3, FWD)
    grad_slices(BWD, 0, 2)
    rs_y(3, BWD)
    grad_slices(BWD, 2, 5)
    leave(rs_x, 2)
    leave(rs_x, 3)
    grad_slices(BWD, 5, 6)
    for copy in pending.values():
        copy.wait_send()


def hand_over(*refs):
    made, results, sems = refs[:4], refs[4:8], refs[8]
    copies = [
        pltpu.make_async_copy(source, result, sems.at[i])
        for i, (source, result) in enumerate(zip(made, results))
    ]
    for copy in copies:
        copy.start()
    for copy in copies:
        copy.wait()


def body(tokens, up_weight, up_mask, down_weight, down_mask, grad_out):
    share, width = tokens.shape
    total = share * lax.axis_size("col")
    part = total // CHUNKS // 8
    piece = share // CHUNKS
    blocks = width // BLOCK
    c = CHUNKS
    hbm = pl.BlockSpec(memory_space=pl.ANY)
    vmem = pl.BlockSpec(memory_space=pltpu.VMEM)
    results = (
        jax.ShapeDtypeStruct((width // HEAD_DIM, share, HEAD_DIM), BF16),
        jax.ShapeDtypeStruct((share, width), BF16),
        jax.ShapeDtypeStruct(up_weight.shape, BF16),
        jax.ShapeDtypeStruct(down_weight.shape, BF16),
    )
    made = pl.pallas_call(
        kernel,
        out_shape=tuple(pltpu.VMEM(r.shape, BF16) for r in results),
        in_specs=[hbm, hbm, vmem, hbm, vmem, hbm],
        out_specs=(vmem,) * 4,
        scratch_shapes=[
            pltpu.VMEM((total, width), BF16),
            pltpu.VMEM((total, width), BF16),
            pltpu.VMEM((width, total), BF16),
            pltpu.VMEM((width, total), BF16),
            pltpu.VMEM(up_weight.shape, BF16),
            pltpu.VMEM(down_weight.shape, BF16),
            pltpu.VMEM((blocks, width), F32),
            pltpu.VMEM((blocks, width), F32),
            pltpu.VMEM((c, 2, 4, part, width), BF16),
            pltpu.VMEM((c, 2, 4, part, width), BF16),
            pltpu.VMEM((c, 4, part, width), BF16),
            pltpu.VMEM((c, 3, 2, part, width), BF16),
            pltpu.VMEM((c, part, width), BF16),
            pltpu.VMEM((c, part, width), F32),
            pltpu.VMEM((c, 3, part, width), BF16),
            pltpu.VMEM((c, part, width), BF16),
            pltpu.VMEM((c, 2, 4, part, width), BF16),
            pltpu.VMEM((c, 2, 4, part, width), BF16),
            pltpu.VMEM((c, 4, 2 * piece, width), BF16),
            pltpu.VMEM((c, 4, 2 * piece, width), BF16),
            pltpu.VMEM((c, 3, 2 * piece, width), BF16),
            pltpu.VMEM((c, 3, 2 * piece, width), BF16),
            pltpu.VMEM((c, 2, piece, width), BF16),
            pltpu.VMEM((c, 2, piece, width), BF16),
            pltpu.VMEM((c, piece, width), BF16),
            pltpu.VMEM((c, piece, width), BF16),
            pltpu.SemaphoreType.DMA((c, MESSAGES)),
            pltpu.SemaphoreType.DMA((c, MESSAGES)),
            pltpu.SemaphoreType.DMA((2 * c + 2,)),
        ],
        compiler_params=pltpu.CompilerParams(
            collective_id=0, has_side_effects=True, vmem_limit_bytes=57000000
        ),
        name="layer",
    )(tokens, up_weight, up_mask, down_weight, down_mask, grad_out)
    return tuple(
        pl.pallas_call(
            hand_over,
            out_shape=results,
            in_specs=[vmem] * 4,
            out_specs=(hbm,) * 4,
            scratch_shapes=[pltpu.SemaphoreType.DMA((4,))],
            compiler_params=pltpu.CompilerParams(vmem_limit_bytes=1 << 20),
            name="hand_over",
        )(*made)
    )


def solution(mesh):
    return jax.shard_map(
        body,
        mesh=mesh,
        in_specs=(
            P("col", "row"),
            P("row", "col"),
            P("row", "col"),
            P("col", "row"),
            P("col", "row"),
            P("col", "row"),
        ),
        out_specs=(P("row", "col", None), P("col", "row"), P("row", "col"), P("col", "row")),
        check_vma=False,
    )
```
